32 devices in a mesh: tm: 4 (over y, core), space: 8 (over z, x).
Axes of the slice: x: 2, y: 2, z: 4, core: 2. Of those that a mesh axis runs over, the one named last changes fastest.
Arguments:
- state_guess: float32 [8, 16, 96, 128], P('tm', 'space'), may hold values from -6 to 6
- adjoint_guess: float32 [8, 16, 96, 128], P('tm', 'space'), may hold values from -6 to 6
- target: float32 [8, 16, 96, 128], P('tm', 'space'), may hold values from -6 to 6
- initial_state: float32 [16, 96, 128], P('space'), may hold values from -6 to 6
- diffusivity: float32 [16, 96, 128], P('space'), may hold values from 0.3 to 3
Outputs:
- state_field: float32 [8, 16, 96, 128], P('tm', 'space')
- adjoint_field: float32 [8, 16, 96, 128], P('tm', 'space')
The draws below stay inside these ranges and needn't reach their ends.
All inputs are finite; a program needn't handle non-finite values.
Results may differ from the reference program's by a relative error of at most 0.00025.
Values sent between devices are 32-bit elements; how exact they have to be, the bound alone decides.
A program may use at most 64 MiB of HBM per device.

```python
import math
import jax
import jax.numpy as jnp

NY = 96
NZ = 128
SWEEPS = 4
OUTER = 2
STEPS = 8
NX = 16


def block_levels(own_key, dims, shards, low, largest):
    gain = 1.0
    for axis_at, blocks in shards:
        heights = jax.random.uniform(jax.random.fold_in(jax.random.fold_in(own_key, 6), axis_at), (blocks,), jnp.float32, low / len(shards), largest / len(shards))
        gain = gain * jnp.repeat(jnp.exp(heights), dims[axis_at] // blocks).reshape((-1,) + (1,) * (len(dims) - 1 - axis_at))
    return gain


def gaussian(stream_key, shape, width, bound, cuts=(), held_as=jnp.bfloat16):
    gain = block_levels(stream_key, shape, cuts, -0.22, 0.18) if cuts else 1.0
    entries = jax.random.normal(stream_key, shape, jnp.float32) * width * gain
    return jnp.minimum(jnp.maximum(entries, -bound), bound).astype(held_as)


def setup_inputs(seed: int = 0) -> dict:
    arg_keys = jax.random.split(jax.random.key(seed), 6)
    return {
        "state_guess": gaussian(arg_keys[0], (STEPS, NX, NY, NZ), 1.0, 6.0, ((0, 4), (1, 8)), jnp.float32),
        "adjoint_guess": gaussian(arg_keys[1], (STEPS, NX, NY, NZ), 1.0, 6.0, ((0, 4), (1, 8)), jnp.float32),
        "target": gaussian(arg_keys[2], (STEPS, NX, NY, NZ), 1.0, 6.0, ((0, 4), (1, 8)), jnp.float32),
        "initial_state": gaussian(arg_keys[3], (NX, NY, NZ), 1.0, 6.0, ((0, 8),), jnp.float32),
        "diffusivity": jnp.clip(jnp.exp(math.log(3.0) - 2.3025851 * jax.random.uniform(arg_keys[4], (NX, NY, NZ), jnp.float32) ** block_levels(arg_keys[4], (NX, NY, NZ), ((0, 8),), -0.2, 0.2)), 0.3, 3.0),
    }


step_size = 0.25
control_cost = 0.05


def rim_slices(padded):
    return [padded[..., 2:, 1:-1, 1:-1], padded[..., :-2, 1:-1, 1:-1],
            padded[..., 1:-1, 2:, 1:-1], padded[..., 1:-1, :-2, 1:-1],
            padded[..., 1:-1, 1:-1, 2:], padded[..., 1:-1, 1:-1, :-2]]


def pad_cells(values):
    widths = [(0, 0)] * (values.ndim - 3) + [(1, 1)] * 3
    return jnp.pad(values, widths)


def face_weights(diffusivity):
    return [0.5 * (diffusivity + beside) for beside in rim_slices(pad_cells(diffusivity))]


def neighbour_sum(values, weights):
    pieces = rim_slices(pad_cells(values))
    summed = weights[0] * pieces[0]
    for weight_one, piece_one in zip(weights[1:], pieces[1:]):
        summed = summed + weight_one * piece_one
    return summed


def apply_block(right_side, shift_real, shift_imag, determinant):
    state_real, state_imag, adjoint_real, adjoint_imag = right_side
    coupling = step_size / control_cost
    new_state_real = (shift_real * state_real + shift_imag * state_imag - coupling * adjoint_real) / determinant
    new_state_imag = (shift_real * state_imag - shift_imag * state_real - coupling * adjoint_imag) / determinant
    new_adjoint_real = (step_size * state_real + shift_real * adjoint_real - shift_imag * adjoint_imag) / determinant
    new_adjoint_imag = (step_size * state_imag + shift_real * adjoint_imag + shift_imag * adjoint_real) / determinant
    return (new_state_real, new_state_imag, new_adjoint_real, new_adjoint_imag)


def reference(state_guess, adjoint_guess, target, initial_state, diffusivity):
    weights = face_weights(diffusivity)
    diagonal = weights[0] + weights[1] + weights[2] + weights[3] + weights[4] + weights[5]
    angles = 2.0 * math.pi * jnp.arange(STEPS, dtype=jnp.float32) / STEPS
    shift_real = (1.0 - jnp.cos(angles))[:, None, None, None] + step_size * diagonal
    shift_imag = jnp.sin(angles)[:, None, None, None]
    determinant = shift_real * shift_real + shift_imag * shift_imag + step_size * step_size / control_cost
    zero_step = jnp.zeros_like(initial_state)[None]
    source = jnp.concatenate([initial_state[None], jnp.zeros_like(state_guess[1:])], 0)
    state_now = state_guess
    adjoint_now = adjoint_guess
    for outer_step in range(OUTER):
        before = jnp.concatenate([zero_step, state_now[:-1]], 0)
        later_adjoint = jnp.concatenate([adjoint_now[1:], zero_step], 0)
        diffuse_state = diagonal * state_now - neighbour_sum(state_now, weights)
        diffuse_adjoint = diagonal * adjoint_now - neighbour_sum(adjoint_now, weights)
        res_state = source - (state_now - before + step_size * diffuse_state + (step_size / control_cost) * adjoint_now)
        res_adjoint = -step_size * target - (adjoint_now - later_adjoint + step_size * diffuse_adjoint - step_size * state_now)
        spec_state = jnp.fft.fft(res_state, axis=0)
        spec_adjoint = jnp.fft.fft(res_adjoint, axis=0)
        right_side = (jnp.real(spec_state), jnp.imag(spec_state), jnp.real(spec_adjoint), jnp.imag(spec_adjoint))
        iterate = apply_block(right_side, shift_real, shift_imag, determinant)
        for sweep_index in range(1, SWEEPS):
            pushed = tuple(side_part + step_size * neighbour_sum(guess_part, weights)
                           for side_part, guess_part in zip(right_side, iterate))
            iterate = apply_block(pushed, shift_real, shift_imag, determinant)
        state_now = state_now + jnp.real(jnp.fft.ifft(iterate[0] + 1j * iterate[1], axis=0))
        adjoint_now = adjoint_now + jnp.real(jnp.fft.ifft(iterate[2] + 1j * iterate[3], axis=0))
    return state_now, adjoint_now
```

```python
import math

import jax
import jax.numpy as jnp
from jax import lax
from jax.experimental import pallas as pl
from jax.experimental.pallas import tpu as pltpu
from jax.sharding import PartitionSpec as P

SWEEPS = 4
OUTER = 2

TAU = 0.25
GAMMA = 0.05
MESH = pl.DeviceIdType.MESH

POOL = 2
PARTS = 4


def turn(pair, angle):
    re, im = pair
    c, s = math.cos(angle), math.sin(angle)
    if im is None:
        return re * c, re * -s
    return re * c + im * s, im * c - re * s


def rfft(xs):
    n = len(xs)
    if n == 1:
        return [(xs[0], None)]
    if n == 2:
        return [(xs[0] + xs[1], None), (xs[0] - xs[1], None)]
    even, odd = rfft(xs[::2]), rfft(xs[1::2])
    out = [None] * (n // 2 + 1)
    out[0] = (even[0][0] + odd[0][0], None)
    out[n // 2] = (even[0][0] - odd[0][0], None)
    out[n // 4] = (even[n // 4][0], -odd[n // 4][0])
    for k in range(1, n // 4):
        er, ei = even[k]
        pr, pi = turn(odd[k], 2.0 * math.pi * k / n)
        out[k] = (er + pr, ei + pi)
        out[n // 2 - k] = (er - pr, pi - ei)
    return out


def irfft(modes):
    n = 2 * (len(modes) - 1)
    if n == 2:
        return [modes[0][0] + modes[1][0], modes[0][0] - modes[1][0]]
    even = [None] * (n // 4 + 1)
    odd = [None] * (n // 4 + 1)
    even[0] = (modes[0][0] + modes[n // 2][0], None)
    odd[0] = (modes[0][0] - modes[n // 2][0], None)
    even[n // 4] = (2.0 * modes[n // 4][0], None)
    odd[n // 4] = (-2.0 * modes[n // 4][1], None)
    for k in range(1, n // 4):
        ar, ai = modes[k]
        br, bi = modes[n // 2 - k]
        even[k] = (ar + br, ai - bi)
        odd[k] = turn((ar - br, ai + bi), -2.0 * math.pi * k / n)
    evens, odds = irfft(even), irfft(odd)
    out = []
    for a, b in zip(evens, odds):
        out += [a, b]
    return out


def make_kernel(T, S, LS, LP, NY, NZ):
    H = T * LS
    G = H // 2
    PX = POOL * T // PARTS
    PXS = PX // POOL
    PL = POOL * LP // PX
    R = NY // PARTS
    W = min(R + 16, NY)
    NXB = (S // POOL) * PX
    f32 = jnp.float32

    def q_of(th, si):
        return 2 * th + lax.rem(si + th, 2)

    def kernel(
        state_in, adjoint_in, target_in, initial_in, kappa_in, state_out, adjoint_out,
        raw, cur, hx, ey, hy, kap, ini, wt, dt, inv, that, fs, a0,
        a2a_send, a2a_recv, one_send, one_recv, ksend, krecv, hsend, hrecv, osend, orecv,
    ):
        t = lax.axis_index("tm")
        s = lax.axis_index("space")
        th, tl = t // PX, lax.rem(t, PX)
        so, si = s // POOL, lax.rem(s, POOL)
        q = q_of(th, si)
        x_at = so * PX + tl
        has = [x_at > 0, x_at < NXB - 1, q > 0, q < PARTS - 1]

        def place_q(qq):
            row = qq // 2
            return row, lax.rem(qq + row, 2)

        def beside(d):
            if d < 2:
                xx = x_at + (1 if d else -1)
                return {"tm": th * PX + lax.rem(xx, PX), "space": (xx // PX) * POOL + si}
            qq = q + (1 if d == 3 else -1)
            row, col = place_q(qq)
            return {"tm": row * PX + tl, "space": so * POOL + col}

        kap[...] = jnp.zeros_like(kap)
        hx[...] = jnp.zeros_like(hx)
        hy[...] = jnp.zeros_like(hy)
        barrier = pltpu.get_barrier_semaphore()
        members = POOL * T
        mine = si * T + t
        for off in range(1, members):
            other = lax.rem(mine + off, members)
            pl.semaphore_signal(
                barrier, inc=1,
                device_id={"tm": lax.rem(other, T), "space": so * POOL + other // T},
                device_id_type=MESH,
            )
        far_left = jnp.logical_and(tl == 0, so > 0)
        far_right = jnp.logical_and(tl == PX - 1, so < S // POOL - 1)
        for d, far in ((0, far_left), (1, far_right)):
            @pl.when(far)
            def _(d=d):
                pl.semaphore_signal(barrier, inc=1, device_id=beside(d), device_id_type=MESH)
        pl.semaphore_wait(
            barrier, members - 1 + jnp.where(far_left, 1, 0) + jnp.where(far_right, 1, 0)
        )

        def send(src, dst, ssem, rsem, tt, ss, wait=False):
            here = jnp.logical_and(tt == t, ss == s)

            @pl.when(here)
            def _():
                if not wait:
                    pltpu.make_async_copy(src, dst, rsem).start()

            @pl.when(jnp.logical_not(here))
            def _():
                copy = pltpu.make_async_remote_copy(
                    src_ref=src, dst_ref=dst, send_sem=ssem, recv_sem=rsem,
                    device_id={"tm": tt, "space": ss}, device_id_type=MESH,
                )
                if wait:
                    copy.wait_send()
                else:
                    copy.start()

        def arrived(dst, rsem):
            pltpu.make_async_copy(dst, dst, rsem).wait()

        def single(wait):
            col = lax.rem(tl, POOL)
            qd = q_of(th, col)
            tt = th * PX + si * PXS + tl // POOL
            ss = so * POOL + col
            planes = pl.ds((tl // POOL) * PL, PL)
            top = pl.multiple_of(jnp.clip(qd * R - 8, 0, NY - W), 8)
            low = pl.multiple_of(top - qd * R + 16, 8)
            send(
                kappa_in.at[planes, pl.ds(top, W)], kap.at[pl.ds(1, PL), pl.ds(low, W)],
                one_send.at[0], one_recv.at[0], tt, ss, wait,
            )
            send(
                initial_in.at[planes, pl.ds(pl.multiple_of(qd * R, 8), R)], ini,
                one_send.at[1], one_recv.at[1], tt, ss, wait,
            )

        def spread(wait):
            for a, source in enumerate((state_in, adjoint_in, target_in)):
                for off in (2, 1, 3, 0):
                    qd = lax.rem(q + off, PARTS)
                    row, col = place_q(qd)
                    for j in range(PXS):
                        tt = row * PX + si * PXS + j
                        send(
                            source.at[:, pl.ds(j * PL, PL), pl.ds(pl.multiple_of(qd * R, 8), R)],
                            raw.at[a, pl.ds(t * LS, LS)],
                            a2a_send.at[a, off, j], a2a_recv.at[a, t], tt, so * POOL + col, wait,
                        )

        single(False)
        spread(False)

        arrived(kap.at[pl.ds(1, PL), pl.ds(0, W)], one_recv.at[0])

        def kappa_copy(d):
            return pltpu.make_async_remote_copy(
                src_ref=kap.at[PL if d else 1, pl.ds(16, R)],
                dst_ref=kap.at[0 if d else PL + 1, pl.ds(16, R)],
                send_sem=ksend.at[d], recv_sem=krecv.at[1 - d],
                device_id=beside(d), device_id_type=MESH,
            )

        for d in (0, 1):
            @pl.when(has[d])
            def _(d=d):
                kappa_copy(d).start()
        for d in (0, 1):
            @pl.when(has[d])
            def _(d=d):
                edge = kap.at[PL + 1 if d else 0, pl.ds(16, R)]
                arrived(edge, krecv.at[d])
                kappa_copy(d).wait_send()

        lane = lax.broadcasted_iota(jnp.int32, (R, NZ), 1)
        for p in range(PL):
            here = kap[p + 1, 16 : 16 + R]
            tall = kap[p + 1, 8 : 24 + R]
            sides = [
                kap[p + 2, 16 : 16 + R],
                kap[p, 16 : 16 + R],
                pltpu.roll(tall, R + 15, 0)[8 : 8 + R],
                pltpu.roll(tall, 1, 0)[8 : 8 + R],
                jnp.where(lane == NZ - 1, 0.0, pltpu.roll(here, NZ - 1, 1)),
                jnp.where(lane == 0, 0.0, pltpu.roll(here, 1, 1)),
            ]
            faces = [0.5 * (here + beside_one) for beside_one in sides]
            total = faces[0]
            for face in faces[1:]:
                total = total + face
            faces[4] = jnp.where(lane == NZ - 1, 0.0, faces[4])
            faces[5] = jnp.where(lane == 0, 0.0, faces[5])
            for i, face in enumerate(faces):
                wt[i, p] = TAU * face
            dt[p] = TAU * total
            for k in range(G + 1):
                angle = 2.0 * math.pi * k / H
                b = math.sin(angle) if 0 < k < G else 0.0
                a = (1.0 - math.cos(angle)) + dt[p]
                inv[k, p] = 1.0 / (a * a + (b * b + TAU * TAU / GAMMA))

        def gather(a):
            for source in range(T):
                arrived(raw.at[a, pl.ds(source * LS, LS)], a2a_recv.at[a, source])

        def paired(modes):
            pairs = [(modes[0][0], modes[G][0])]
            for k in range(1, G):
                pairs.append(modes[k])
            return pairs

        def rows_out(par, g, v, p, value):
            ey[par, 0, g, v * PL + p : v * PL + p + 1] = value[0:1]
            ey[par, 1, g, v * PL + p : v * PL + p + 1] = value[R - 1 : R]

        def halo_copy(par, d, g):
            if d < 2:
                src = cur.at[par, g, :, PL - 1 if d else 0]
                dst = hx.at[par, 1 - d, g]
            else:
                src = ey.at[par, d - 2, g]
                dst = hy.at[par, 3 - d, g]
            return pltpu.make_async_remote_copy(
                src_ref=src, dst_ref=dst,
                send_sem=hsend.at[par, d, g], recv_sem=hrecv.at[par, d ^ 1, g],
                device_id=beside(d), device_id_type=MESH,
            )

        def halo_start(par, g, dirs=(0, 1, 2, 3)):
            for d in dirs:
                @pl.when(has[d])
                def _(d=d):
                    halo_copy(par, d, g).start()

        def halo_wait(par, g):
            for d in range(4):
                @pl.when(has[d])
                def _(d=d):
                    dst = hx.at[par, d, g] if d < 2 else hy.at[par, d - 2, g]
                    arrived(dst, hrecv.at[par, d, g])
                    halo_copy(par, d, g).wait_send()

        for a in range(2):
            gather(a)
            for p in range(PL):
                pairs = paired(rfft([raw[a, n, p] for n in range(H)]))
                for g, pair in enumerate(pairs):
                    for i in range(2):
                        cur[0, g, 2 * a + i, p] = pair[i]
                        rows_out(0, g, 2 * a + i, p, pair[i])
        for g in range(G):
            halo_start(0, g)
        arrived(ini, one_recv.at[1])
        for p in range(PL):
            fs[p] = ini[p] - raw[0, H - 1, p]
            a0[p] = raw[1, 0, p]
        gather(2)
        for p in range(PL):
            pairs = paired(rfft([raw[2, n, p] for n in range(H)]))
            for g, pair in enumerate(pairs):
                for i in range(2):
                    that[g, i, p] = -TAU * pair[i]
        single(True)
        spread(True)

        row_at = lax.broadcasted_iota(jnp.int32, (R, NZ), 0)
        coupling = TAU / GAMMA

        def spread_sum(par, g, v, p, weights):
            c = cur[par, g, v, p]
            left = hx[par, 0, g, v] if p == 0 else cur[par, g, v, p - 1]
            right = hx[par, 1, g, v] if p == PL - 1 else cur[par, g, v, p + 1]
            at = v * PL + p
            above = jnp.where(row_at == 0, hy[par, 0, g, at : at + 1], pltpu.roll(c, 1, 0))
            below = jnp.where(row_at == R - 1, hy[par, 1, g, at : at + 1], pltpu.roll(c, R - 1, 0))
            out = weights[0] * right + weights[1] * left
            out = out + (weights[2] * below + weights[3] * above)
            return out + (
                weights[4] * pltpu.roll(c, NZ - 1, 1) + weights[5] * pltpu.roll(c, 1, 1)
            )

        def sweep(par, g):
            nxt = 1 - par
            for p in range(PL):
                weights = [wt[i, p] for i in range(6)]
                ua, ub, pa, pb = [spread_sum(par, g, v, p, weights) for v in range(4)]
                ua = ua + fs[p]
                if g == 0:
                    ub = ub + fs[p]
                    pa = pa + (that[g, 0, p] - a0[p])
                    pb = pb + (that[g, 1, p] + a0[p])
                    low, high = dt[p], 2.0 + dt[p]
                    new = [
                        (low * ua - coupling * pa) * inv[0, p],
                        (high * ub - coupling * pb) * inv[G, p],
                        (TAU * ua + low * pa) * inv[0, p],
                        (TAU * ub + high * pb) * inv[G, p],
                    ]
                else:
                    c, b = math.cos(2.0 * math.pi * g / H), math.sin(2.0 * math.pi * g / H)
                    pa = pa + (that[g, 0, p] - c * a0[p])
                    pb = pb + (that[g, 1, p] - b * a0[p])
                    a = (1.0 - c) + dt[p]
                    scale = inv[g, p]
                    new = [
                        (a * ua + b * ub - coupling * pa) * scale,
                        (a * ub - b * ua - coupling * pb) * scale,
                        (TAU * ua + a * pa - b * pb) * scale,
                        (TAU * ub + a * pb + b * pa) * scale,
                    ]
                for v in range(4):
                    cur[nxt, g, v, p] = new[v]
                    rows_out(nxt, g, v, p, new[v])

        for outer in range(OUTER):
            start = outer * SWEEPS
            if outer:
                par = start % 2
                for p in range(PL):
                    last = cur[par, 0, 0, p] - cur[par, 0, 1, p]
                    first = cur[par, 0, 2, p] + cur[par, 0, 3, p]
                    for g in range(1, G):
                        angle = 2.0 * math.pi * g / H
                        last = last + (2.0 * math.cos(angle)) * cur[par, g, 0, p]
                        last = last + (2.0 * math.sin(angle)) * cur[par, g, 1, p]
                        first = first + 2.0 * cur[par, g, 2, p]
                    fs[p] = ini[p] - last * (1.0 / H)
                    a0[p] = first * (1.0 / H)

            def body(i, carry, start=start):
                par = lax.rem(start + i, 2)
                for g in range(G):
                    halo_wait(par, g)
                    sweep(par, g)

                    @pl.when(start + i < OUTER * SWEEPS - 1)
                    def _(g=g):
                        halo_start(1 - par, g)
                return carry

            lax.fori_loop(0, SWEEPS, body, 0)

        par = (OUTER * SWEEPS) % 2
        si_to = (tl * PL) // LP
        at_plane = tl * PL - si_to * LP

        def deliver(a, wait):
            for off in range(T):
                tt = lax.rem(t + T - 1 - off, T)
                out = (state_out, adjoint_out)[a]
                send(
                    raw.at[a, pl.ds(tt * LS, LS)],
                    out.at[:, pl.ds(at_plane, PL), pl.ds(pl.multiple_of(q * R, 8), R)],
                    osend.at[a, off], orecv.at[a, q, tl - si_to * PXS], tt, so * POOL + si_to, wait,
                )

        for a in range(2):
            for p in range(PL):
                fields = [[cur[par, g, 2 * a + i, p] for i in range(2)] for g in range(G)]
                modes = [(fields[0][0], None)] + [tuple(f) for f in fields[1:]]
                modes.append((fields[0][1], None))
                for n, value in enumerate(irfft(modes)):
                    raw[a, n, p] = value * (1.0 / H)
            deliver(a, False)
        for a, out in enumerate((state_out, adjoint_out)):
            for qq in range(PARTS):
                for j in range(PXS):
                    arrived(
                        out.at[:, pl.ds(j * PL, PL), pl.ds(qq * R, R)], orecv.at[a, qq, j]
                    )
            deliver(a, True)

    dma = pltpu.SemaphoreType.DMA
    scratch = [
        pltpu.VMEM((3, H, PL, R, NZ), f32),
        pltpu.VMEM((2, G, 4, PL, R, NZ), f32),
        pltpu.VMEM((2, 2, G, 4, R, NZ), f32),
        pltpu.VMEM((2, 2, G, 4 * PL, NZ), f32),
        pltpu.VMEM((2, 2, G, 4 * PL, NZ), f32),
        pltpu.VMEM((PL + 2, R + 32, NZ), f32),
        pltpu.VMEM((PL, R, NZ), f32),
        pltpu.VMEM((6, PL, R, NZ), f32),
        pltpu.VMEM((PL, R, NZ), f32),
        pltpu.VMEM((G + 1, PL, R, NZ), f32),
        pltpu.VMEM((G, 2, PL, R, NZ), f32),
        pltpu.VMEM((PL, R, NZ), f32),
        pltpu.VMEM((PL, R, NZ), f32),
        dma((3, PARTS, PXS)),
        dma((3, T)),
        dma((2,)),
        dma((2,)),
        dma((2,)),
        dma((2,)),
        dma((2, 4, G)),
        dma((2, 4, G)),
        dma((2, T)),
        dma((2, PARTS, PXS)),
    ]
    return kernel, scratch


def solution(mesh):
    T, S = mesh.shape["tm"], mesh.shape["space"]

    def on_device(state_guess, adjoint_guess, target, initial_state, diffusivity):
        LS, LP, NY, NZ = state_guess.shape
        kernel, scratch = make_kernel(T, S, LS, LP, NY, NZ)
        shape = jax.ShapeDtypeStruct(state_guess.shape, jnp.float32)
        return pl.pallas_call(
            kernel,
            out_shape=(shape, shape),
            in_specs=[pl.BlockSpec(memory_space=pl.ANY)] * 5,
            out_specs=[pl.BlockSpec(memory_space=pl.ANY)] * 2,
            scratch_shapes=scratch,
            compiler_params=pltpu.CompilerParams(collective_id=0, has_side_effects=True),
        )(state_guess, adjoint_guess, target, initial_state, diffusivity)

    field = P("tm", "space", None, None)
    cells = P("space", None, None)
    return jax.shard_map(
        on_device, mesh=mesh, in_specs=(field, field, field, cells, cells),
        out_specs=(field, field), check_vma=False,
    )
```

```python
import math

import jax
import jax.numpy as jnp
from jax import lax
from jax.experimental import pallas as pl
from jax.experimental.pallas import tpu as pltpu
from jax.sharding import PartitionSpec as P

SWEEPS = 4
OUTER = 2

TAU = 0.25
GAMMA = 0.05
MESH = pl.DeviceIdType.MESH

POOL = 2
PARTS = 4


def turn(pair, angle):
    re, im = pair
    c, s = math.cos(angle), math.sin(angle)
    if im is None:
        return re * c, re * -s
    return re * c + im * s, im * c - re * s


def rfft(xs):
    n = len(xs)
    if n == 1:
        return [(xs[0], None)]
    if n == 2:
        return [(xs[0] + xs[1], None), (xs[0] - xs[1], None)]
    even, odd = rfft(xs[::2]), rfft(xs[1::2])
    out = [None] * (n // 2 + 1)
    out[0] = (even[0][0] + odd[0][0], None)
    out[n // 2] = (even[0][0] - odd[0][0], None)
    out[n // 4] = (even[n // 4][0], -odd[n // 4][0])
    for k in range(1, n // 4):
        er, ei = even[k]
        pr, pi = turn(odd[k], 2.0 * math.pi * k / n)
        out[k] = (er + pr, ei + pi)
        out[n // 2 - k] = (er - pr, pi - ei)
    return out


def irfft(modes):
    n = 2 * (len(modes) - 1)
    if n == 2:
        return [modes[0][0] + modes[1][0], modes[0][0] - modes[1][0]]
    even = [None] * (n // 4 + 1)
    odd = [None] * (n // 4 + 1)
    even[0] = (modes[0][0] + modes[n // 2][0], None)
    odd[0] = (modes[0][0] - modes[n // 2][0], None)
    even[n // 4] = (2.0 * modes[n // 4][0], None)
    odd[n // 4] = (-2.0 * modes[n // 4][1], None)
    for k in range(1, n // 4):
        ar, ai = modes[k]
        br, bi = modes[n // 2 - k]
        even[k] = (ar + br, ai - bi)
        odd[k] = turn((ar - br, ai + bi), -2.0 * math.pi * k / n)
    evens, odds = irfft(even), irfft(odd)
    out = []
    for a, b in zip(evens, odds):
        out += [a, b]
    return out


def make_kernel(T, S, LS, LP, NY, NZ):
    H = T * LS
    G = H // 2
    PX = POOL * T // PARTS
    PXS = PX // POOL
    PL = POOL * LP // PX
    R = NY // PARTS
    W = min(R + 16, NY)
    NXB = (S // POOL) * PX
    f32 = jnp.float32

    def q_of(th, si):
        return 2 * th + lax.rem(si + th, 2)

    def kernel(
        state_in, adjoint_in, target_in, initial_in, kappa_in, state_out, adjoint_out,
        raw, cur, hx, ey, hy, kap, ini, wt, dt, inv, that, fs, a0,
        a2a_send, a2a_recv, one_send, one_recv, ksend, krecv, hsend, hrecv, osend, orecv,
    ):
        t = lax.axis_index("tm")
        s = lax.axis_index("space")
        th, tl = t // PX, lax.rem(t, PX)
        so, si = s // POOL, lax.rem(s, POOL)
        q = q_of(th, si)
        x_at = so * PX + tl
        has = [x_at > 0, x_at < NXB - 1, q > 0, q < PARTS - 1]

        def place_q(qq):
            row = qq // 2
            return row, lax.rem(qq + row, 2)

        def beside(d):
            if d < 2:
                xx = x_at + (1 if d else -1)
                return {"tm": th * PX + lax.rem(xx, PX), "space": (xx // PX) * POOL + si}
            qq = q + (1 if d == 3 else -1)
            row, col = place_q(qq)
            return {"tm": row * PX + tl, "space": so * POOL + col}

        kap[...] = jnp.zeros_like(kap)
        barrier = pltpu.get_barrier_semaphore()
        members = POOL * T
        mine = si * T + t
        for off in range(1, members):
            other = lax.rem(mine + off, members)
            pl.semaphore_signal(
                barrier, inc=1,
                device_id={"tm": lax.rem(other, T), "space": so * POOL + other // T},
                device_id_type=MESH,
            )
        far_left = jnp.logical_and(tl == 0, so > 0)
        far_right = jnp.logical_and(tl == PX - 1, so < S // POOL - 1)
        for d, far in ((0, far_left), (1, far_right)):
            @pl.when(far)
            def _(d=d):
                pl.semaphore_signal(barrier, inc=1, device_id=beside(d), device_id_type=MESH)
        pl.semaphore_wait(
            barrier, members - 1 + jnp.where(far_left, 1, 0) + jnp.where(far_right, 1, 0)
        )

        def send(src, dst, ssem, rsem, tt, ss, wait=False):
            here = jnp.logical_and(tt == t, ss == s)

            @pl.when(here)
            def _():
                if not wait:
                    pltpu.make_async_copy(src, dst, rsem).start()

            @pl.when(jnp.logical_not(here))
            def _():
                copy = pltpu.make_async_remote_copy(
                    src_ref=src, dst_ref=dst, send_sem=ssem, recv_sem=rsem,
                    device_id={"tm": tt, "space": ss}, device_id_type=MESH,
                )
                if wait:
                    copy.wait_send()
                else:
                    copy.start()

        def arrived(dst, rsem):
            pltpu.make_async_copy(dst, dst, rsem).wait()

        def single(wait):
            col = lax.rem(tl, POOL)
            qd = q_of(th, col)
            tt = th * PX + si * PXS + tl // POOL
            ss = so * POOL + col
            planes = pl.ds((tl // POOL) * PL, PL)
            top = pl.multiple_of(jnp.clip(qd * R - 8, 0, NY - W), 8)
            low = pl.multiple_of(top - qd * R + 16, 8)
            send(
                kappa_in.at[planes, pl.ds(top, W)], kap.at[pl.ds(1, PL), pl.ds(low, W)],
                one_send.at[0], one_recv.at[0], tt, ss, wait,
            )
            send(
                initial_in.at[planes, pl.ds(pl.multiple_of(qd * R, 8), R)], ini,
                one_send.at[1], one_recv.at[1], tt, ss, wait,
            )

        def spread(wait):
            for a, source in enumerate((state_in, adjoint_in, target_in)):
                for off in (2, 1, 3, 0):
                    qd = lax.rem(q + off, PARTS)
                    row, col = place_q(qd)
                    for j in range(PXS):
                        tt = row * PX + si * PXS + j
                        send(
                            source.at[:, pl.ds(j * PL, PL), pl.ds(pl.multiple_of(qd * R, 8), R)],
                            raw.at[a, pl.ds(t * LS, LS)],
                            a2a_send.at[a, off, j], a2a_recv.at[a, t], tt, so * POOL + col, wait,
                        )

        single(False)
        spread(False)

        for d, edges in enumerate((hx, hx, hy, hy)):
            @pl.when(jnp.logical_not(has[d]))
            def _(d=d, edges=edges):
                for par in range(2):
                    edges[par, d % 2] = jnp.zeros(edges.shape[2:], f32)

        arrived(kap.at[pl.ds(1, PL), pl.ds(0, W)], one_recv.at[0])

        def kappa_copy(d):
            return pltpu.make_async_remote_copy(
                src_ref=kap.at[PL if d else 1, pl.ds(16, R)],
                dst_ref=kap.at[0 if d else PL + 1, pl.ds(16, R)],
                send_sem=ksend.at[d], recv_sem=krecv.at[1 - d],
                device_id=beside(d), device_id_type=MESH,
            )

        for d in (0, 1):
            @pl.when(has[d])
            def _(d=d):
                kappa_copy(d).start()
        for d in (0, 1):
            @pl.when(has[d])
            def _(d=d):
                edge = kap.at[PL + 1 if d else 0, pl.ds(16, R)]
                arrived(edge, krecv.at[d])
                kappa_copy(d).wait_send()

        lane = lax.broadcasted_iota(jnp.int32, (R, NZ), 1)
        for p in range(PL):
            here = kap[p + 1, 16 : 16 + R]
            tall = kap[p + 1, 8 : 24 + R]
            sides = [
                kap[p + 2, 16 : 16 + R],
                kap[p, 16 : 16 + R],
                pltpu.roll(tall, R + 15, 0)[8 : 8 + R],
                pltpu.roll(tall, 1, 0)[8 : 8 + R],
                jnp.where(lane == NZ - 1, 0.0, pltpu.roll(here, NZ - 1, 1)),
                jnp.where(lane == 0, 0.0, pltpu.roll(here, 1, 1)),
            ]
            faces = [0.5 * (here + beside_one) for beside_one in sides]
            total = faces[0]
            for face in faces[1:]:
                total = total + face
            faces[4] = jnp.where(lane == NZ - 1, 0.0, faces[4])
            faces[5] = jnp.where(lane == 0, 0.0, faces[5])
            for i, face in enumerate(faces):
                wt[i, p] = TAU * face
            dt[p] = TAU * total
            for k in range(G + 1):
                angle = 2.0 * math.pi * k / H
                b = math.sin(angle) if 0 < k < G else 0.0
                a = (1.0 - math.cos(angle)) + dt[p]
                inv[k, p] = 1.0 / (a * a + (b * b + TAU * TAU / GAMMA))

        def gather(a):
            for source in range(T):
                arrived(raw.at[a, pl.ds(source * LS, LS)], a2a_recv.at[a, source])

        def paired(modes):
            pairs = [(modes[0][0], modes[G][0])]
            for k in range(1, G):
                pairs.append(modes[k])
            return pairs

        def rows_out(par, g, v, p, value):
            ey[par, 0, g, v * PL + p : v * PL + p + 1] = value[0:1]
            ey[par, 1, g, v * PL + p : v * PL + p + 1] = value[R - 1 : R]

        def halo_copy(par, d, g):
            if d < 2:
                src = cur.at[par, g, :, PL - 1 if d else 0]
                dst = hx.at[par, 1 - d, g]
            else:
                src = ey.at[par, d - 2, g]
                dst = hy.at[par, 3 - d, g]
            return pltpu.make_async_remote_copy(
                src_ref=src, dst_ref=dst,
                send_sem=hsend.at[par, d, g], recv_sem=hrecv.at[par, d ^ 1, g],
                device_id=beside(d), device_id_type=MESH,
            )

        def halo_start(par, g, dirs=(0, 1, 2, 3)):
            for d in dirs:
                @pl.when(has[d])
                def _(d=d):
                    halo_copy(par, d, g).start()

        def halo_wait(par, g):
            for d in range(4):
                @pl.when(has[d])
                def _(d=d):
                    dst = hx.at[par, d, g] if d < 2 else hy.at[par, d - 2, g]
                    arrived(dst, hrecv.at[par, d, g])

        def halo_sent(par, g):
            for d in range(4):
                @pl.when(has[d])
                def _(d=d):
                    halo_copy(par, d, g).wait_send()

        for a in range(2):
            gather(a)
            for p in range(PL):
                pairs = paired(rfft([raw[a, n, p] for n in range(H)]))
                for g, pair in enumerate(pairs):
                    for i in range(2):
                        cur[0, g, 2 * a + i, p] = pair[i]
                        rows_out(0, g, 2 * a + i, p, pair[i])
        for g in range(G):
            halo_start(0, g)
        arrived(ini, one_recv.at[1])
        for p in range(PL):
            fs[p] = ini[p] - raw[0, H - 1, p]
            a0[p] = raw[1, 0, p]
        gather(2)
        for p in range(PL):
            pairs = paired(rfft([raw[2, n, p] for n in range(H)]))
            for g, pair in enumerate(pairs):
                for i in range(2):
                    that[g, i, p] = -TAU * pair[i]
        single(True)
        spread(True)

        row_at = lax.broadcasted_iota(jnp.int32, (R, NZ), 0)
        coupling = TAU / GAMMA

        def spread_sum(par, g, v, p, weights):
            c = cur[par, g, v, p]
            left = hx[par, 0, g, v] if p == 0 else cur[par, g, v, p - 1]
            right = hx[par, 1, g, v] if p == PL - 1 else cur[par, g, v, p + 1]
            at = v * PL + p
            above = jnp.where(row_at == 0, hy[par, 0, g, at : at + 1], pltpu.roll(c, 1, 0))
            below = jnp.where(row_at == R - 1, hy[par, 1, g, at : at + 1], pltpu.roll(c, R - 1, 0))
            out = weights[0] * right + weights[1] * left
            out = out + (weights[2] * below + weights[3] * above)
            return out + (
                weights[4] * pltpu.roll(c, NZ - 1, 1) + weights[5] * pltpu.roll(c, 1, 1)
            )

        def sweep(par, g):
            nxt = 1 - par
            for p in range(PL):
                weights = [wt[i, p] for i in range(6)]
                ua, ub, pa, pb = [spread_sum(par, g, v, p, weights) for v in range(4)]
                ua = ua + fs[p]
                if g == 0:
                    ub = ub + fs[p]
                    pa = pa + (that[g, 0, p] - a0[p])
                    pb = pb + (that[g, 1, p] + a0[p])
                    low, high = dt[p], 2.0 + dt[p]
                    new = [
                        (low * ua - coupling * pa) * inv[0, p],
                        (high * ub - coupling * pb) * inv[G, p],
                        (TAU * ua + low * pa) * inv[0, p],
                        (TAU * ub + high * pb) * inv[G, p],
                    ]
                else:
                    c, b = math.cos(2.0 * math.pi * g / H), math.sin(2.0 * math.pi * g / H)
                    pa = pa + (that[g, 0, p] - c * a0[p])
                    pb = pb + (that[g, 1, p] - b * a0[p])
                    a = (1.0 - c) + dt[p]
                    scale = inv[g, p]
                    new = [
                        (a * ua + b * ub - coupling * pa) * scale,
                        (a * ub - b * ua - coupling * pb) * scale,
                        (TAU * ua + a * pa - b * pb) * scale,
                        (TAU * ub + a * pb + b * pa) * scale,
                    ]
                for v in range(4):
                    cur[nxt, g, v, p] = new[v]
                    rows_out(nxt, g, v, p, new[v])

        for outer in range(OUTER):
            start = outer * SWEEPS
            if outer:
                par = start % 2
                for p in range(PL):
                    last = cur[par, 0, 0, p] - cur[par, 0, 1, p]
                    first = cur[par, 0, 2, p] + cur[par, 0, 3, p]
                    for g in range(1, G):
                        angle = 2.0 * math.pi * g / H
                        last = last + (2.0 * math.cos(angle)) * cur[par, g, 0, p]
                        last = last + (2.0 * math.sin(angle)) * cur[par, g, 1, p]
                        first = first + 2.0 * cur[par, g, 2, p]
                    fs[p] = ini[p] - last * (1.0 / H)
                    a0[p] = first * (1.0 / H)

            def body(i, carry, start=start):
                par = lax.rem(start + i, 2)
                for g in range(G):
                    halo_wait(par, g)

                    @pl.when(start + i > 0)
                    def _(g=g):
                        halo_sent(1 - par, g)

                    sweep(par, g)

                    @pl.when(start + i < OUTER * SWEEPS - 1)
                    def _(g=g):
                        halo_start(1 - par, g)
                return carry

            lax.fori_loop(0, SWEEPS, body, 0)

        par = (OUTER * SWEEPS) % 2
        for g in range(G):
            halo_sent(1 - par, g)
        si_to = (tl * PL) // LP
        at_plane = tl * PL - si_to * LP

        def deliver(a, wait):
            for off in range(T):
                row, col = (T - 1 - off) // PX, (T - 1 - off) % PX
                tt = lax.rem(th + row, T // PX) * PX + lax.rem(tl + col, PX)
                out = (state_out, adjoint_out)[a]
                send(
                    raw.at[a, pl.ds(tt * LS, LS)],
                    out.at[:, pl.ds(at_plane, PL), pl.ds(pl.multiple_of(q * R, 8), R)],
                    osend.at[a, off], orecv.at[a, q, tl - si_to * PXS], tt, so * POOL + si_to, wait,
                )

        for a in range(2):
            for p in range(PL):
                fields = [[cur[par, g, 2 * a + i, p] for i in range(2)] for g in range(G)]
                modes = [(fields[0][0], None)] + [tuple(f) for f in fields[1:]]
                modes.append((fields[0][1], None))
                for n, value in enumerate(irfft(modes)):
                    raw[a, n, p] = value
            deliver(a, False)
        for a, out in enumerate((state_out, adjoint_out)):
            for qq in range(PARTS):
                for j in range(PXS):
                    arrived(
                        out.at[:, pl.ds(j * PL, PL), pl.ds(qq * R, R)], orecv.at[a, qq, j]
                    )
            deliver(a, True)

    dma = pltpu.SemaphoreType.DMA
    scratch = [
        pltpu.VMEM((3, H, PL, R, NZ), f32),
        pltpu.VMEM((2, G, 4, PL, R, NZ), f32),
        pltpu.VMEM((2, 2, G, 4, R, NZ), f32),
        pltpu.VMEM((2, 2, G, 4 * PL, NZ), f32),
        pltpu.VMEM((2, 2, G, 4 * PL, NZ), f32),
        pltpu.VMEM((PL + 2, R + 32, NZ), f32),
        pltpu.VMEM((PL, R, NZ), f32),
        pltpu.VMEM((6, PL, R, NZ), f32),
        pltpu.VMEM((PL, R, NZ), f32),
        pltpu.VMEM((G + 1, PL, R, NZ), f32),
        pltpu.VMEM((G, 2, PL, R, NZ), f32),
        pltpu.VMEM((PL, R, NZ), f32),
        pltpu.VMEM((PL, R, NZ), f32),
        dma((3, PARTS, PXS)),
        dma((3, T)),
        dma((2,)),
        dma((2,)),
        dma((2,)),
        dma((2,)),
        dma((2, 4, G)),
        dma((2, 4, G)),
        dma((2, T)),
        dma((2, PARTS, PXS)),
    ]
    return kernel, scratch


def solution(mesh):
    T, S = mesh.shape["tm"], mesh.shape["space"]

    def on_device(state_guess, adjoint_guess, target, initial_state, diffusivity):
        LS, LP, NY, NZ = state_guess.shape
        kernel, scratch = make_kernel(T, S, LS, LP, NY, NZ)
        outs = pl.pallas_call(
            kernel,
            out_shape=(pltpu.VMEM(state_guess.shape, jnp.float32),) * 2,
            in_specs=[pl.BlockSpec(memory_space=pl.ANY)] * 5,
            out_specs=[pl.BlockSpec(memory_space=pltpu.VMEM)] * 2,
            scratch_shapes=scratch,
            compiler_params=pltpu.CompilerParams(collective_id=0, has_side_effects=True),
        )(state_guess, adjoint_guess, target, initial_state, diffusivity)
        return outs[0] * (1.0 / (T * LS)), outs[1] * (1.0 / (T * LS))

    field = P("tm", "space", None, None)
    cells = P("space", None, None)
    return jax.shard_map(
        on_device, mesh=mesh, in_specs=(field, field, field, cells, cells),
        out_specs=(field, field), check_vma=False,
    )
```

```python
import math

import jax
import jax.numpy as jnp
from jax import lax
from jax.experimental import pallas as pl
from jax.experimental.pallas import tpu as pltpu
from jax.sharding import PartitionSpec as P

SWEEPS = 4
OUTER = 2

TAU = 0.25
GAMMA = 0.05
MESH = pl.DeviceIdType.MESH

POOL = 2
PARTS = 4


def turn(pair, angle):
    re, im = pair
    c, s = math.cos(angle), math.sin(angle)
    if im is None:
        return re * c, re * -s
    return re * c + im * s, im * c - re * s


def rfft(xs):
    n = len(xs)
    if n == 1:
        return [(xs[0], None)]
    if n == 2:
        return [(xs[0] + xs[1], None), (xs[0] - xs[1], None)]
    even, odd = rfft(xs[::2]), rfft(xs[1::2])
    out = [None] * (n // 2 + 1)
    out[0] = (even[0][0] + odd[0][0], None)
    out[n // 2] = (even[0][0] - odd[0][0], None)
    out[n // 4] = (even[n // 4][0], -odd[n // 4][0])
    for k in range(1, n // 4):
        er, ei = even[k]
        pr, pi = turn(odd[k], 2.0 * math.pi * k / n)
        out[k] = (er + pr, ei + pi)
        out[n // 2 - k] = (er - pr, pi - ei)
    return out


def irfft(modes):
    n = 2 * (len(modes) - 1)
    if n == 2:
        return [modes[0][0] + modes[1][0], modes[0][0] - modes[1][0]]
    even = [None] * (n // 4 + 1)
    odd = [None] * (n // 4 + 1)
    even[0] = (modes[0][0] + modes[n // 2][0], None)
    odd[0] = (modes[0][0] - modes[n // 2][0], None)
    even[n // 4] = (2.0 * modes[n // 4][0], None)
    odd[n // 4] = (-2.0 * modes[n // 4][1], None)
    for k in range(1, n // 4):
        ar, ai = modes[k]
        br, bi = modes[n // 2 - k]
        even[k] = (ar + br, ai - bi)
        odd[k] = turn((ar - br, ai + bi), -2.0 * math.pi * k / n)
    evens, odds = irfft(even), irfft(odd)
    out = []
    for a, b in zip(evens, odds):
        out += [a, b]
    return out


def make_kernel(T, S, LS, LP, NY, NZ):
    H = T * LS
    G = H // 2
    PX = POOL * T // PARTS
    PXS = PX // POOL
    PL = POOL * LP // PX
    R = NY // PARTS
    W = min(R + 16, NY)
    NXB = (S // POOL) * PX
    f32 = jnp.float32

    def q_of(th, si):
        return 2 * th + lax.rem(si + th, 2)

    def kernel(
        state_in, adjoint_in, target_in, initial_in, kappa_in, state_out, adjoint_out,
        raw, cur, hx, ey, hy, kap, ini, wt, dt, inv, that, fs, a0,
        a2a_send, a2a_recv, one_send, one_recv, ksend, krecv, hsend, hrecv, osend, orecv,
    ):
        t = lax.axis_index("tm")
        s = lax.axis_index("space")
        th, tl = t // PX, lax.rem(t, PX)
        so, si = s // POOL, lax.rem(s, POOL)
        q = q_of(th, si)
        x_at = so * PX + tl
        has = [x_at > 0, x_at < NXB - 1, q > 0, q < PARTS - 1]

        def place_q(qq):
            row = qq // 2
            return row, lax.rem(qq + row, 2)

        def beside(d):
            if d < 2:
                xx = x_at + (1 if d else -1)
                return {"tm": th * PX + lax.rem(xx, PX), "space": (xx // PX) * POOL + si}
            qq = q + (1 if d == 3 else -1)
            row, col = place_q(qq)
            return {"tm": row * PX + tl, "space": so * POOL + col}

        kap[...] = jnp.zeros_like(kap)
        barrier = pltpu.get_barrier_semaphore()
        members = POOL * T
        mine = si * T + t
        for off in range(1, members):
            other = lax.rem(mine + off, members)
            pl.semaphore_signal(
                barrier, inc=1,
                device_id={"tm": lax.rem(other, T), "space": so * POOL + other // T},
                device_id_type=MESH,
            )
        far_left = jnp.logical_and(tl == 0, so > 0)
        far_right = jnp.logical_and(tl == PX - 1, so < S // POOL - 1)
        for d, far in ((0, far_left), (1, far_right)):
            @pl.when(far)
            def _(d=d):
                pl.semaphore_signal(barrier, inc=1, device_id=beside(d), device_id_type=MESH)
        pl.semaphore_wait(
            barrier, members - 1 + jnp.where(far_left, 1, 0) + jnp.where(far_right, 1, 0)
        )

        def send(src, dst, ssem, rsem, tt, ss, wait=False):
            here = jnp.logical_and(tt == t, ss == s)

            @pl.when(here)
            def _():
                if not wait:
                    pltpu.make_async_copy(src, dst, rsem).start()

            @pl.when(jnp.logical_not(here))
            def _():
                copy = pltpu.make_async_remote_copy(
                    src_ref=src, dst_ref=dst, send_sem=ssem, recv_sem=rsem,
                    device_id={"tm": tt, "space": ss}, device_id_type=MESH,
                )
                if wait:
                    copy.wait_send()
                else:
                    copy.start()

        def arrived(dst, rsem):
            pltpu.make_async_copy(dst, dst, rsem).wait()

        def single(wait, kappa=True, initial=True):
            col = lax.rem(tl, POOL)
            qd = q_of(th, col)
            tt = th * PX + si * PXS + tl // POOL
            ss = so * POOL + col
            planes = pl.ds((tl // POOL) * PL, PL)
            top = pl.multiple_of(jnp.clip(qd * R - 8, 0, NY - W), 8)
            low = pl.multiple_of(top - qd * R + 16, 8)
            if kappa:
                send(
                    kappa_in.at[planes, pl.ds(top, W)], kap.at[pl.ds(1, PL), pl.ds(low, W)],
                    one_send.at[0], one_recv.at[0], tt, ss, wait,
                )
            if initial:
                send(
                    initial_in.at[planes, pl.ds(pl.multiple_of(qd * R, 8), R)], ini,
                    one_send.at[1], one_recv.at[1], tt, ss, wait,
                )

        def spread(wait):
            for a, source in enumerate((state_in, adjoint_in, target_in)):
                for off in (2, 1, 3, 0):
                    qd = lax.rem(q + off, PARTS)
                    row, col = place_q(qd)
                    for j in range(PXS):
                        tt = row * PX + si * PXS + j
                        send(
                            source.at[:, pl.ds(j * PL, PL), pl.ds(pl.multiple_of(qd * R, 8), R)],
                            raw.at[a, pl.ds(t * LS, LS)],
                            a2a_send.at[a, off, j], a2a_recv.at[a, t], tt, so * POOL + col, wait,
                        )

        single(False, initial=False)
        spread(False)
        single(False, kappa=False)

        for d, edges in enumerate((hx, hx, hy, hy)):
            @pl.when(jnp.logical_not(has[d]))
            def _(d=d, edges=edges):
                for par in range(2):
                    edges[par, d % 2] = jnp.zeros(edges.shape[2:], f32)

        arrived(kap.at[pl.ds(1, PL), pl.ds(0, W)], one_recv.at[0])

        def kappa_copy(d):
            return pltpu.make_async_remote_copy(
                src_ref=kap.at[PL if d else 1, pl.ds(16, R)],
                dst_ref=kap.at[0 if d else PL + 1, pl.ds(16, R)],
                send_sem=ksend.at[d], recv_sem=krecv.at[1 - d],
                device_id=beside(d), device_id_type=MESH,
            )

        for d in (0, 1):
            @pl.when(has[d])
            def _(d=d):
                kappa_copy(d).start()
        for d in (0, 1):
            @pl.when(has[d])
            def _(d=d):
                edge = kap.at[PL + 1 if d else 0, pl.ds(16, R)]
                arrived(edge, krecv.at[d])
                kappa_copy(d).wait_send()

        lane = lax.broadcasted_iota(jnp.int32, (R, NZ), 1)
        for p in range(PL):
            here = kap[p + 1, 16 : 16 + R]
            tall = kap[p + 1, 8 : 24 + R]
            sides = [
                kap[p + 2, 16 : 16 + R],
                kap[p, 16 : 16 + R],
                pltpu.roll(tall, R + 15, 0)[8 : 8 + R],
                pltpu.roll(tall, 1, 0)[8 : 8 + R],
                jnp.where(lane == NZ - 1, 0.0, pltpu.roll(here, NZ - 1, 1)),
                jnp.where(lane == 0, 0.0, pltpu.roll(here, 1, 1)),
            ]
            faces = [0.5 * (here + beside_one) for beside_one in sides]
            total = faces[0]
            for face in faces[1:]:
                total = total + face
            faces[4] = jnp.where(lane == NZ - 1, 0.0, faces[4])
            faces[5] = jnp.where(lane == 0, 0.0, faces[5])
            for i, face in enumerate(faces):
                wt[i, p] = TAU * face
            dt[p] = TAU * total
            for k in range(G + 1):
                angle = 2.0 * math.pi * k / H
                b = math.sin(angle) if 0 < k < G else 0.0
                a = (1.0 - math.cos(angle)) + dt[p]
                inv[k, p] = 1.0 / (a * a + (b * b + TAU * TAU / GAMMA))

        def gather(a):
            for source in range(T):
                arrived(raw.at[a, pl.ds(source * LS, LS)], a2a_recv.at[a, source])

        def paired(modes):
            pairs = [(modes[0][0], modes[G][0])]
            for k in range(1, G):
                pairs.append(modes[k])
            return pairs

        def rows_out(par, g, v, p, value):
            ey[par, 0, g, v * PL + p : v * PL + p + 1] = value[0:1]
            ey[par, 1, g, v * PL + p : v * PL + p + 1] = value[R - 1 : R]

        def halo_copy(par, d, g):
            if d < 2:
                src = cur.at[par, g, :, PL - 1 if d else 0]
                dst = hx.at[par, 1 - d, g]
            else:
                src = ey.at[par, d - 2, g]
                dst = hy.at[par, 3 - d, g]
            return pltpu.make_async_remote_copy(
                src_ref=src, dst_ref=dst,
                send_sem=hsend.at[par, d, g], recv_sem=hrecv.at[par, d ^ 1, g],
                device_id=beside(d), device_id_type=MESH,
            )

        def halo_start(par, g, dirs=(0, 1, 2, 3)):
            for d in dirs:
                @pl.when(has[d])
                def _(d=d):
                    halo_copy(par, d, g).start()

        def halo_wait(par, g):
            for d in range(4):
                @pl.when(has[d])
                def _(d=d):
                    dst = hx.at[par, d, g] if d < 2 else hy.at[par, d - 2, g]
                    arrived(dst, hrecv.at[par, d, g])

        def halo_sent(par, g):
            for d in range(4):
                @pl.when(has[d])
                def _(d=d):
                    halo_copy(par, d, g).wait_send()

        for a in range(2):
            gather(a)
            for p in range(PL):
                pairs = paired(rfft([raw[a, n, p] for n in range(H)]))
                for g, pair in enumerate(pairs):
                    for i in range(2):
                        cur[0, g, 2 * a + i, p] = pair[i]
                        rows_out(0, g, 2 * a + i, p, pair[i])
        for g in range(G):
            halo_start(0, g)
        gather(2)
        for p in range(PL):
            pairs = paired(rfft([raw[2, n, p] for n in range(H)]))
            for g, pair in enumerate(pairs):
                for i in range(2):
                    that[g, i, p] = -TAU * pair[i]
        arrived(ini, one_recv.at[1])
        for p in range(PL):
            fs[p] = ini[p] - raw[0, H - 1, p]
            a0[p] = raw[1, 0, p]
        single(True)
        spread(True)

        row_at = lax.broadcasted_iota(jnp.int32, (R, NZ), 0)
        coupling = TAU / GAMMA

        def spread_sum(par, g, v, p, weights):
            c = cur[par, g, v, p]
            left = hx[par, 0, g, v] if p == 0 else cur[par, g, v, p - 1]
            right = hx[par, 1, g, v] if p == PL - 1 else cur[par, g, v, p + 1]
            at = v * PL + p
            above = jnp.where(row_at == 0, hy[par, 0, g, at : at + 1], pltpu.roll(c, 1, 0))
            below = jnp.where(row_at == R - 1, hy[par, 1, g, at : at + 1], pltpu.roll(c, R - 1, 0))
            out = weights[0] * right + weights[1] * left
            out = out + (weights[2] * below + weights[3] * above)
            return out + (
                weights[4] * pltpu.roll(c, NZ - 1, 1) + weights[5] * pltpu.roll(c, 1, 1)
            )

        def sweep(par, g):
            nxt = 1 - par
            for p in range(PL):
                weights = [wt[i, p] for i in range(6)]
                ua, ub, pa, pb = [spread_sum(par, g, v, p, weights) for v in range(4)]
                ua = ua + fs[p]
                if g == 0:
                    ub = ub + fs[p]
                    pa = pa + (that[g, 0, p] - a0[p])
                    pb = pb + (that[g, 1, p] + a0[p])
                    low, high = dt[p], 2.0 + dt[p]
                    new = [
                        (low * ua - coupling * pa) * inv[0, p],
                        (high * ub - coupling * pb) * inv[G, p],
                        (TAU * ua + low * pa) * inv[0, p],
                        (TAU * ub + high * pb) * inv[G, p],
                    ]
                else:
                    c, b = math.cos(2.0 * math.pi * g / H), math.sin(2.0 * math.pi * g / H)
                    pa = pa + (that[g, 0, p] - c * a0[p])
                    pb = pb + (that[g, 1, p] - b * a0[p])
                    a = (1.0 - c) + dt[p]
                    scale = inv[g, p]
                    new = [
                        (a * ua + b * ub - coupling * pa) * scale,
                        (a * ub - b * ua - coupling * pb) * scale,
                        (TAU * ua + a * pa - b * pb) * scale,
                        (TAU * ub + a * pb + b * pa) * scale,
                    ]
                for v in range(4):
                    cur[nxt, g, v, p] = new[v]
                    rows_out(nxt, g, v, p, new[v])

        for outer in range(OUTER):
            start = outer * SWEEPS
            if outer:
                par = start % 2
                for p in range(PL):
                    last = cur[par, 0, 0, p] - cur[par, 0, 1, p]
                    first = cur[par, 0, 2, p] + cur[par, 0, 3, p]
                    for g in range(1, G):
                        angle = 2.0 * math.pi * g / H
                        last = last + (2.0 * math.cos(angle)) * cur[par, g, 0, p]
                        last = last + (2.0 * math.sin(angle)) * cur[par, g, 1, p]
                        first = first + 2.0 * cur[par, g, 2, p]
                    fs[p] = ini[p] - last * (1.0 / H)
                    a0[p] = first * (1.0 / H)

            def body(i, carry, start=start):
                par = lax.rem(start + i, 2)
                for g in range(G):
                    halo_wait(par, g)

                    @pl.when(start + i > 0)
                    def _(g=g):
                        halo_sent(1 - par, g)

                    sweep(par, g)

                    @pl.when(start + i < OUTER * SWEEPS - 1)
                    def _(g=g):
                        halo_start(1 - par, g)
                return carry

            lax.fori_loop(0, SWEEPS, body, 0)

        par = (OUTER * SWEEPS) % 2
        for g in range(G):
            halo_sent(1 - par, g)
        si_to = (tl * PL) // LP
        at_plane = tl * PL - si_to * LP

        def deliver(a, wait):
            for off in range(T):
                row, col = (T - 1 - off) // PX, (T - 1 - off) % PX
                tt = lax.rem(th + row, T // PX) * PX + lax.rem(tl + col, PX)
                out = (state_out, adjoint_out)[a]
                send(
                    raw.at[a, pl.ds(tt * LS, LS)],
                    out.at[:, pl.ds(at_plane, PL), pl.ds(pl.multiple_of(q * R, 8), R)],
                    osend.at[a, off], orecv.at[a, q, tl - si_to * PXS], tt, so * POOL + si_to, wait,
                )

        for a in range(2):
            for p in range(PL):
                fields = [[cur[par, g, 2 * a + i, p] for i in range(2)] for g in range(G)]
                modes = [(fields[0][0], None)] + [tuple(f) for f in fields[1:]]
                modes.append((fields[0][1], None))
                for n, value in enumerate(irfft(modes)):
                    raw[a, n, p] = value
            deliver(a, False)
        for a, out in enumerate((state_out, adjoint_out)):
            for qq in range(PARTS):
                for j in range(PXS):
                    arrived(
                        out.at[:, pl.ds(j * PL, PL), pl.ds(qq * R, R)], orecv.at[a, qq, j]
                    )
            deliver(a, True)

    dma = pltpu.SemaphoreType.DMA
    scratch = [
        pltpu.VMEM((3, H, PL, R, NZ), f32),
        pltpu.VMEM((2, G, 4, PL, R, NZ), f32),
        pltpu.VMEM((2, 2, G, 4, R, NZ), f32),
        pltpu.VMEM((2, 2, G, 4 * PL, NZ), f32),
        pltpu.VMEM((2, 2, G, 4 * PL, NZ), f32),
        pltpu.VMEM((PL + 2, R + 32, NZ), f32),
        pltpu.VMEM((PL, R, NZ), f32),
        pltpu.VMEM((6, PL, R, NZ), f32),
        pltpu.VMEM((PL, R, NZ), f32),
        pltpu.VMEM((G + 1, PL, R, NZ), f32),
        pltpu.VMEM((G, 2, PL, R, NZ), f32),
        pltpu.VMEM((PL, R, NZ), f32),
        pltpu.VMEM((PL, R, NZ), f32),
        dma((3, PARTS, PXS)),
        dma((3, T)),
        dma((2,)),
        dma((2,)),
        dma((2,)),
        dma((2,)),
        dma((2, 4, G)),
        dma((2, 4, G)),
        dma((2, T)),
        dma((2, PARTS, PXS)),
    ]
    return kernel, scratch


def solution(mesh):
    T, S = mesh.shape["tm"], mesh.shape["space"]

    def on_device(state_guess, adjoint_guess, target, initial_state, diffusivity):
        LS, LP, NY, NZ = state_guess.shape
        kernel, scratch = make_kernel(T, S, LS, LP, NY, NZ)
        outs = pl.pallas_call(
            kernel,
            out_shape=(pltpu.VMEM(state_guess.shape, jnp.float32),) * 2,
            in_specs=[pl.BlockSpec(memory_space=pl.ANY)] * 5,
            out_specs=[pl.BlockSpec(memory_space=pltpu.VMEM)] * 2,
            scratch_shapes=scratch,
            compiler_params=pltpu.CompilerParams(collective_id=0, has_side_effects=True),
        )(state_guess, adjoint_guess, target, initial_state, diffusivity)
        return outs[0] * (1.0 / (T * LS)), outs[1] * (1.0 / (T * LS))

    field = P("tm", "space", None, None)
    cells = P("space", None, None)
    return jax.shard_map(
        on_device, mesh=mesh, in_specs=(field, field, field, cells, cells),
        out_specs=(field, field), check_vma=False,
    )
```
